512 devices in a mesh: tok: 128 (over y, z, core), head: 4 (over x).
Axes of the slice: x: 4, y: 4, z: 16, core: 2. Of those that a mesh axis runs over, the one named last changes fastest.
Arguments:
- queries: bfloat16 [4, 32768, 256], P('head', 'tok'), may hold values from -5 to 5
- key_vectors: bfloat16 [4, 32768, 256], P('head', 'tok'), may hold values from -5 to 5
- value_vectors: bfloat16 [4, 32768, 256], P('head', 'tok'), may hold values from -8 to 8
- token_rate: float32 [4, 32768], P('head', 'tok'), may hold values from 0.1 to 1
- fast_gate: bfloat16 [4, 512, 256], P('head'), may hold values from -0.375 to 0.375
- fast_up: bfloat16 [4, 512, 256], P('head'), may hold values from -0.375 to 0.375
- fast_down: bfloat16 [4, 512, 256], P('head'), may hold values from -0.25 to 0.25
- attention_gain: float32 [4, 256], P('head'), may hold values from 0.25 to 1.75
- memory_gain: float32 [4, 256], P('head'), may hold values from 0.25 to 1.75
Outputs:
- layer_output: bfloat16 [4, 32768, 256], P('head', 'tok')
The draws below stay inside these ranges and needn't reach their ends.
All inputs are finite; a program needn't handle non-finite values.
Results may differ from the reference program's by a relative error of at most 0.0065.
Values may be sent and summed in bfloat16 or wider, within the bound.
No kernel may reach another device: no remote copies, remote signals or barrier semaphores. Data moves between devices by JAX's collectives and lax.ppermute only.
A program may use at most 64 MiB of HBM per device.

```python
import math
import jax
import jax.numpy as jnp
from jax import lax

DH = 256
FH = 512
HEADS = 4
BLOCK = 256
HALO = 128
NS_STEPS = 2
TOK_DEV = 256
TOKENS = 32768


def drawn_entries(key, full_shape):
    return jnp.clip(jax.random.normal(key, full_shape, jnp.float32), -4.0, 4.0)


def draw_queries(key, part):
    matrix_elements = drawn_entries(jax.random.fold_in(key, 1), (HEADS, TOKENS, DH))
    return matrix_elements.astype(jnp.bfloat16)


def draw_key_vectors(key, part):
    matrix_elements = drawn_entries(jax.random.fold_in(key, 2), (HEADS, TOKENS, DH))
    return matrix_elements.astype(jnp.bfloat16)


def draw_value_vectors(key, part):
    head_index = jnp.arange(HEADS, dtype=jnp.float32)[:, None, None]
    head_level = 0.6 * 3.0 ** (head_index / (HEADS - 1))
    return (drawn_entries(jax.random.fold_in(key, 3), (HEADS, TOKENS, DH)) * head_level).astype(jnp.bfloat16)


def levels(key, dims, shards, low, top_value):
    def one(axis_at, parts):
        steps = jax.random.uniform(jax.random.fold_in(jax.random.fold_in(key, 6), axis_at), (parts,), jnp.float32, low / len(shards), top_value / len(shards))
        return jnp.repeat(jnp.exp(steps), dims[axis_at] // parts).reshape((-1,) + (1,) * (len(dims) - axis_at - 1))

    factor_of = one(*shards[0])
    for cut in shards[1:]:
        factor_of = factor_of * one(*cut)
    return factor_of


def gaussian(own_key, shape, scale, reach, shards=(), held_as=jnp.bfloat16):
    result = jax.random.normal(own_key, shape, jnp.float32) * scale
    if len(shards) > 0:
        result = levels(own_key, shape, shards, -0.22, 0.18) * result
    return jnp.clip(result, min=-reach, max=reach).astype(held_as)


def setup_inputs(seed: int = 0) -> dict:
    seeds = jax.random.split(jax.random.key(seed), 10)
    queries = draw_queries(jax.random.fold_in(seeds[9], 71), 0)
    key_vectors = draw_key_vectors(jax.random.fold_in(seeds[9], 71), 0)
    value_vectors = draw_value_vectors(jax.random.fold_in(seeds[9], 71), 0)
    token_rate = jnp.clip(jnp.exp(math.log(1.0) - 2.3025851 * jax.random.uniform(seeds[3], (HEADS, TOKENS), jnp.float32) ** levels(seeds[3], (HEADS, TOKENS), ((0, 4), (1, 128)), -0.2, 0.2)), 0.1, 1.0)
    fast_gate = gaussian(seeds[4], (HEADS, FH, DH), DH ** -0.5, 0.375, ((0, 4),))
    fast_up = gaussian(seeds[5], (HEADS, FH, DH), DH ** -0.5, 0.375, ((0, 4),))
    fast_down = gaussian(seeds[6], (HEADS, FH, DH), FH ** -0.5, 0.25, ((0, 4),))
    attention_gain = jnp.clip(1.0 + 0.15 * jax.random.normal(seeds[7], (HEADS, DH), jnp.float32), 0.25, 1.75)
    memory_gain = jnp.clip(1.0 + 0.15 * jax.random.normal(seeds[8], (HEADS, DH), jnp.float32), 0.25, 1.75)
    return dict(queries=queries, key_vectors=key_vectors, value_vectors=value_vectors, token_rate=token_rate, fast_gate=fast_gate, fast_up=fast_up, fast_down=fast_down, attention_gain=attention_gain, memory_gain=memory_gain)


first_coeff = 3.4445
second_coeff = -4.775
third_coefficient = 2.0315
step_size = 1.0
norm_floor = 1e-07
epsilon = 1e-06
masked_score = -1e+30

def window_attention(probe_matrix_lines, key_rows, value_rows):
    margin_zeros = jnp.zeros((HALO, DH), key_rows.dtype)
    padded_keys = jnp.concatenate([margin_zeros, key_rows, margin_zeros], axis=0)
    padded_values = jnp.concatenate([margin_zeros, value_rows, margin_zeros], axis=0)

    def single_segment(block_index):
        offset = block_index * BLOCK
        block_queries = lax.dynamic_slice_in_dim(probe_matrix_lines, offset, BLOCK, 0)
        neighbourhood_lookup_vectors = lax.dynamic_slice_in_dim(padded_keys, offset, 2 * BLOCK, 0)
        windowed_values = lax.dynamic_slice_in_dim(padded_values, offset, 2 * BLOCK, 0)
        scores = jnp.dot(block_queries, neighbourhood_lookup_vectors.T, preferred_element_type=jnp.float32) * DH ** (-0.5)
        positions = offset - HALO + jnp.arange(2 * BLOCK, dtype=jnp.int32)
        inside = (positions >= 0) & (positions < TOKENS)
        scores = jnp.where(inside[None, :], scores, masked_score)
        highest = lax.optimization_barrier(jnp.max(scores, axis=1, keepdims=True))
        weights = jnp.exp(scores - highest)
        denominator = lax.optimization_barrier(jnp.sum(weights, axis=1, keepdims=True))
        attention_probabilities = (weights / denominator).astype(jnp.bfloat16)
        return jnp.dot(attention_probabilities, windowed_values, preferred_element_type=jnp.float32)
    blocks = lax.map(single_segment, jnp.arange(TOKENS // BLOCK, dtype=jnp.int32))
    return blocks.reshape(TOKENS, DH)

def fast_gradients(key_rows, value_rows, rates, gate_weights, up_weights, down_weights):

    def add_piece(totals, piece_index):
        offset = piece_index * TOK_DEV
        keys_here = lax.dynamic_slice_in_dim(key_rows, offset, TOK_DEV, 0)
        values_here = lax.dynamic_slice_in_dim(value_rows, offset, TOK_DEV, 0)
        rates_here = lax.dynamic_slice_in_dim(rates, offset, TOK_DEV, 0)
        gate_value = jnp.dot(keys_here, gate_weights.T, preferred_element_type=jnp.float32)
        up_value = jnp.dot(keys_here, up_weights.T, preferred_element_type=jnp.float32)
        squashed = jax.nn.sigmoid(gate_value)
        hidden = (gate_value * squashed * up_value).astype(jnp.bfloat16)
        scaled = (rates_here[:, None] * values_here.astype(jnp.float32)).astype(jnp.bfloat16)
        reverse_pass = jnp.dot(scaled, down_weights.T, preferred_element_type=jnp.float32)
        gate_grad = (reverse_pass * up_value * squashed * (1.0 + gate_value * (1.0 - squashed))).astype(jnp.bfloat16)
        up_grad = (reverse_pass * gate_value * squashed).astype(jnp.bfloat16)
        grad_gate = jnp.dot(gate_grad.T, keys_here, preferred_element_type=jnp.float32)
        grad_up = jnp.dot(up_grad.T, keys_here, preferred_element_type=jnp.float32)
        grad_down = jnp.dot(hidden.T, scaled, preferred_element_type=jnp.float32)
        return ((totals[0] + grad_gate, totals[1] + grad_up, totals[2] + grad_down), None)
    zeros = jnp.zeros((FH, DH), jnp.float32)
    totals, unused = lax.scan(add_piece, (zeros, zeros, zeros), jnp.arange(TOKENS // TOK_DEV, dtype=jnp.int32))
    return totals

def newton_schulz(gradient):
    magnitude = jnp.sqrt(jnp.sum(gradient * gradient))
    current = gradient / (magnitude + norm_floor)
    for iteration in range(NS_STEPS):
        product = jnp.dot(current.T, current, precision=lax.Precision.HIGHEST)
        squared = jnp.dot(product, product, precision=lax.Precision.HIGHEST)
        mixer = second_coeff * product + third_coefficient * squared
        current = first_coeff * current + jnp.dot(current, mixer, precision=lax.Precision.HIGHEST)
    return current

def reference(queries, key_vectors, value_vectors, token_rate, fast_gate, fast_up, fast_down, attention_gain, memory_gain):
    attended_heads = []
    memory_heads = []
    for head_index in range(HEADS):
        attended_heads.append(window_attention(queries[head_index], key_vectors[head_index], value_vectors[head_index]))
        grads = fast_gradients(key_vectors[head_index], value_vectors[head_index], token_rate[head_index], fast_gate[head_index], fast_up[head_index], fast_down[head_index])
        renewed = []
        for weights, gradient in zip((fast_gate[head_index], fast_up[head_index], fast_down[head_index]), grads):
            renewed.append((weights.astype(jnp.float32) + step_size * newton_schulz(gradient)).astype(jnp.bfloat16))
        gate_value = jnp.dot(queries[head_index], renewed[0].T, preferred_element_type=jnp.float32)
        up_value = jnp.dot(queries[head_index], renewed[1].T, preferred_element_type=jnp.float32)
        memory_hidden = (jax.nn.silu(gate_value) * up_value).astype(jnp.bfloat16)
        memory_heads.append(jnp.dot(memory_hidden, renewed[2], preferred_element_type=jnp.float32))
    attended = jnp.stack(attended_heads)
    memory = jnp.stack(memory_heads)
    width_mean = lax.optimization_barrier(jnp.mean(attended * attended, axis=(0, 2)))
    attention_part = attended * lax.rsqrt(width_mean + epsilon)[None, :, None] * attention_gain[:, None, :]
    memory_mean = lax.optimization_barrier(jnp.mean(memory * memory, axis=2, keepdims=True))
    memory_part = memory * lax.rsqrt(memory_mean + epsilon) * memory_gain[:, None, :]
    return (attention_part + memory_part).astype(jnp.bfloat16)
```

```python
import jax
import jax.numpy as jnp
from jax import lax
from jax.sharding import Mesh
from jax.sharding import PartitionSpec as P

BLOCK = 256
HALO = 128
NS_STEPS = 2
TOK = ("y", "zh", "zl", "c")
NEAR = ("y", "zl")
FAR = "zh"
PAIR = "c"

first_coeff = 3.4445
second_coeff = -4.775
third_coefficient = 2.0315
step_size = 1.0
norm_floor = 1e-07
epsilon = 1e-06
masked_score = -1e30


def dot(a, b, dims, precision=None):
    return lax.dot_general(
        a, b, (dims, ((), ())), precision=precision, preferred_element_type=jnp.float32
    )


def outer_halo(keys, values, core):
    count = lax.axis_size(TOK)
    swap = [(i, i + 1) for i in range(1, count - 1, 2)] + [(i + 1, i) for i in range(1, count - 1, 2)]
    stacked = jnp.stack([keys, values])
    edge = jnp.where(core == 0, stacked[:, :HALO], stacked[:, -HALO:])
    return lax.ppermute(edge, TOK, swap)


def copies_to(array, axis):
    copies = jnp.broadcast_to(array, (lax.axis_size(axis), *array.shape))
    return lax.all_to_all(copies, axis, split_axis=0, concat_axis=0, tiled=True)


def window_attention(queries, pair_keys, pair_values, outer, core, has_outer):
    head_depth = queries.shape[1]
    start = core * HALO
    width = 2 * BLOCK - HALO
    keys = lax.dynamic_slice_in_dim(pair_keys, start, width, 0)
    values = lax.dynamic_slice_in_dim(pair_values, start, width, 0)
    scale = head_depth ** (-0.5)
    inner = dot(queries, keys, ((1,), (1,))) * scale
    outside = dot(queries, outer[0], ((1,), (1,))) * scale
    outside = jnp.where(has_outer, outside, masked_score)
    highest = jnp.maximum(
        jnp.max(inner, axis=1, keepdims=True), jnp.max(outside, axis=1, keepdims=True)
    )
    inner = jnp.exp(inner - highest)
    outside = jnp.exp(outside - highest)
    total = jnp.sum(inner, axis=1, keepdims=True) + jnp.sum(outside, axis=1, keepdims=True)
    inner = (inner / total).astype(jnp.bfloat16)
    outside = (outside / total).astype(jnp.bfloat16)
    return dot(inner, values, ((1,), (0,))) + dot(outside, outer[1], ((1,), (0,)))


def fast_gradients(keys, scaled, gate_weights, up_weights, down_weights):
    gate_value = dot(keys, gate_weights, ((1,), (1,)))
    up_value = dot(keys, up_weights, ((1,), (1,)))
    squashed = jax.nn.sigmoid(gate_value)
    hidden = (gate_value * squashed * up_value).astype(jnp.bfloat16)
    backward = dot(scaled, down_weights, ((1,), (1,)))
    gate_grad = (backward * up_value * squashed * (1.0 + gate_value * (1.0 - squashed))).astype(
        jnp.bfloat16
    )
    up_grad = (backward * gate_value * squashed).astype(jnp.bfloat16)
    return jnp.concatenate(
        [
            dot(gate_grad, keys, ((0,), (0,))).astype(jnp.bfloat16),
            dot(up_grad, keys, ((0,), (0,))).astype(jnp.bfloat16),
            dot(hidden, scaled, ((0,), (0,))).astype(jnp.bfloat16),
        ],
        axis=1,
    )


def sum_over_tokens(grads):
    near = lax.axis_size(NEAR)
    tiles = grads.reshape(near, -1, grads.shape[1])
    arrived = lax.all_to_all(tiles, NEAR, split_axis=0, concat_axis=0, tiled=True)
    own = jnp.sum(arrived.astype(jnp.float32), axis=0).astype(jnp.bfloat16)
    own = jnp.sum(copies_to(own, FAR).astype(jnp.float32), axis=0).astype(jnp.bfloat16)
    half = copies_to(own, NEAR).reshape(grads.shape)
    return lax.all_gather(half, PAIR, axis=0, tiled=True)


def orthogonalize(grad):
    grad = grad.astype(jnp.float32)
    current = grad * (1.0 / (jnp.sqrt(jnp.sum(grad * grad)) + norm_floor))
    for iteration in range(NS_STEPS):
        product = dot(current, current, ((0,), (0,)), lax.Precision.HIGH)
        squared = dot(product, product, ((1,), (0,)), lax.Precision.HIGH)
        mixer = second_coeff * product + third_coefficient * squared
        current = first_coeff * current + dot(current, mixer, ((1,), (0,)), lax.Precision.HIGH)
    return current


def on_device(
    queries,
    key_vectors,
    value_vectors,
    token_rate,
    fast_gate,
    fast_up,
    fast_down,
    attention_gain,
    memory_gain,
):
    queries, keys, values = queries[0], key_vectors[0], value_vectors[0]
    rates = token_rate[0]
    head_depth = queries.shape[1]
    hidden_units = fast_gate.shape[1]
    core = lax.axis_index(PAIR)
    index = lax.axis_index(TOK)
    has_outer = jnp.where(core == 0, index > 0, index < lax.axis_size(TOK) - 1)

    scaled = (rates[:, None] * values.astype(jnp.float32)).astype(jnp.bfloat16)
    pair = lax.all_gather(jnp.stack([keys, scaled, values]), PAIR, axis=1, tiled=True)
    half = hidden_units // 2
    mine = [
        lax.dynamic_slice_in_dim(w[0], core * half, half, 0) for w in (fast_gate, fast_up, fast_down)
    ]
    grads = fast_gradients(pair[0], pair[1], *mine)
    summed = sum_over_tokens(grads)

    outer = outer_halo(keys, values, core)
    attended = window_attention(queries, pair[0], pair[2], outer, core, has_outer)
    squares = jnp.sum(attended * attended, axis=1)
    width_sum = jnp.sum(copies_to(squares.reshape(1, -1), "head"), axis=0)[0]
    width_mean = width_sum / (lax.axis_size("head") * head_depth)
    attention_part = attended * lax.rsqrt(width_mean + epsilon)[:, None] * attention_gain

    renewed = []
    for i, w in enumerate((fast_gate, fast_up, fast_down)):
        update = orthogonalize(summed[:, i * head_depth : (i + 1) * head_depth])
        renewed.append((w[0].astype(jnp.float32) + step_size * update).astype(jnp.bfloat16))
    gate_value = dot(queries, renewed[0], ((1,), (1,)))
    up_value = dot(queries, renewed[1], ((1,), (1,)))
    memory_hidden = (jax.nn.silu(gate_value) * up_value).astype(jnp.bfloat16)
    memory = dot(memory_hidden, renewed[2], ((1,), (0,)))
    memory_mean = jnp.mean(memory * memory, axis=1, keepdims=True)
    memory_part = memory * lax.rsqrt(memory_mean + epsilon) * memory_gain
    return (attention_part + memory_part).astype(jnp.bfloat16)[None]


def solution(mesh):
    finer = Mesh(
        mesh.devices.reshape(4, 4, 4, 2, mesh.shape["head"]), ("y", "zh", "zl", "c", "head")
    )
    return jax.shard_map(
        on_device,
        mesh=finer,
        in_specs=(
            P("head", TOK, None),
            P("head", TOK, None),
            P("head", TOK, None),
            P("head", TOK),
            P("head", None, None),
            P("head", None, None),
            P("head", None, None),
            P("head", None),
            P("head", None),
        ),
        out_specs=P("head", TOK, None),
        check_vma=False,
    )
```

```python
import functools

import jax
import jax.numpy as jnp
from jax import lax
from jax.experimental import pallas as pl
from jax.experimental.pallas import tpu as pltpu
from jax.sharding import Mesh
from jax.sharding import PartitionSpec as P


HALO = 128
NS_STEPS = 2
TOK = ("y", "zh", "zl", "c")
NEAR = ("y", "zl")
FAR = "zh"
PAIR = "c"

first_coeff = 3.4445
second_coeff = -4.775
third_coefficient = 2.0315
step_size = 1.0
norm_floor = 1e-07
epsilon = 1e-06
masked_score = -1e30

VMEM = pl.BlockSpec(memory_space=pltpu.VMEM)
SMEM = pl.BlockSpec(memory_space=pltpu.SMEM)


def dot(a, b, dims):
    return lax.dot_general(a, b, (dims, ((), ())), preferred_element_type=jnp.float32)


def outer_halo(keys, values, core):
    count = lax.axis_size(TOK)
    ends = range(1, count - 1, 2)
    swap = [(i, i + 1) for i in ends] + [(i + 1, i) for i in ends]
    first = jnp.stack([keys[:HALO], values[:HALO]])
    last = jnp.stack([keys[-HALO:], values[-HALO:]])
    return lax.ppermute(jnp.where(core == 0, first, last), TOK, swap)


def from_partner(array):
    return lax.ppermute(array, PAIR, [(0, 1), (1, 0)])


def exchange(tiles, axis):
    return lax.all_to_all(tiles, axis, split_axis=0, concat_axis=0, tiled=True)


def copies_to(array, axis):
    copies = jnp.broadcast_to(array, (lax.axis_size(axis), *array.shape))
    return exchange(copies, axis)


def head_sum(partial):
    heads = lax.axis_size("head")
    distance = 1
    while distance < heads:
        pairs = [(i, i ^ distance) for i in range(heads)]
        partial = partial + lax.ppermute(partial, "head", pairs)
        distance *= 2
    return partial


def window_attention(queries, keys, values, partner_keys, partner_values, outer, core, has_outer):
    head_depth = queries.shape[1]
    near_keys = lax.dynamic_slice_in_dim(partner_keys, core * HALO, HALO, 0)
    near_values = lax.dynamic_slice_in_dim(partner_values, core * HALO, HALO, 0)
    scale = head_depth ** (-0.5)
    scores = [dot(queries, k, ((1,), (1,))) * scale for k in (keys, near_keys, outer[0])]
    scores[2] = jnp.where(has_outer, scores[2], masked_score)
    highest = functools.reduce(jnp.maximum, [jnp.max(s, axis=1, keepdims=True) for s in scores])
    weights = [jnp.exp(s - highest) for s in scores]
    total = sum(jnp.sum(w, axis=1, keepdims=True) for w in weights)
    parts = [
        dot((w / total).astype(jnp.bfloat16), v, ((1,), (0,)))
        for w, v in zip(weights, (values, near_values, outer[1]))
    ]
    return parts[0] + parts[1] + parts[2]


def gradient_kernel(core_ref, own_ref, partner_ref, gate_ref, up_ref, down_ref, out_ref):
    half = out_ref.shape[0]
    depth = gate_ref.shape[2]
    mine = pl.ds(pl.multiple_of(core_ref[0] * half, half), half)
    gate_weights, up_weights, down_weights = gate_ref[0, mine], up_ref[0, mine], down_ref[0, mine]
    sums = [0.0, 0.0, 0.0]
    for ref in (own_ref, partner_ref):
        keys, scaled = ref[0], ref[1]
        gate_value = dot(keys, gate_weights, ((1,), (1,)))
        up_value = dot(keys, up_weights, ((1,), (1,)))
        backward = dot(scaled, down_weights, ((1,), (1,)))
        squashed = jax.nn.sigmoid(gate_value)
        silu = gate_value * squashed
        hidden = (silu * up_value).astype(jnp.bfloat16)
        gate_grad = (
            backward * up_value * squashed * (1.0 + gate_value * (1.0 - squashed))
        ).astype(jnp.bfloat16)
        up_grad = (backward * silu).astype(jnp.bfloat16)
        sums[0] += dot(gate_grad, keys, ((0,), (0,)))
        sums[1] += dot(up_grad, keys, ((0,), (0,)))
        sums[2] += dot(hidden, scaled, ((0,), (0,)))
    for i, total in enumerate(sums):
        out_ref[:, i * depth : (i + 1) * depth] = total.astype(jnp.bfloat16)


def renew_kernel(
    core_ref,
    own_ref,
    partner_ref,
    gate_ref,
    up_ref,
    down_ref,
    queries_ref,
    attention_ref,
    gain_ref,
    out_ref,
):
    half = own_ref.shape[0]
    depth = gate_ref.shape[2]
    core = core_ref[0]
    rows = [pl.ds(pl.multiple_of(c * half, half), half) for c in (core, 1 - core)]
    renewed = []
    for i, weights_ref in enumerate((gate_ref, up_ref, down_ref)):
        grads = [ref[:, i * depth : (i + 1) * depth] for ref in (own_ref, partner_ref)]
        wide = [g.astype(jnp.float32) for g in grads]
        squares = jnp.sum(wide[0] * wide[0] + wide[1] * wide[1], axis=0, keepdims=True)
        norm = jnp.sqrt(jnp.sum(squares, axis=1, keepdims=True))
        scaling = 1.0 / (norm + norm_floor)
        current = [g * scaling for g in wide]
        for _ in range(NS_STEPS):
            rounded = [c.astype(jnp.bfloat16) for c in current]
            product = sum(dot(c, c, ((0,), (0,))) for c in rounded)
            low = product.astype(jnp.bfloat16)
            squared = dot(low, low, ((1,), (0,)))
            mixer = (second_coeff * product + third_coefficient * squared).astype(jnp.bfloat16)
            current = [
                first_coeff * c + dot(r, mixer, ((1,), (0,))) for c, r in zip(current, rounded)
            ]
        renewed.append(
            [
                (weights_ref[0, r].astype(jnp.float32) + step_size * c).astype(jnp.bfloat16)
                for r, c in zip(rows, current)
            ]
        )
    queries = queries_ref[0]
    memory = 0.0
    for gate_weights, up_weights, down_weights in zip(*renewed):
        gate_value = dot(queries, gate_weights, ((1,), (1,)))
        up_value = dot(queries, up_weights, ((1,), (1,)))
        hidden = (gate_value * jax.nn.sigmoid(gate_value) * up_value).astype(jnp.bfloat16)
        memory += dot(hidden, down_weights, ((1,), (0,)))
    mean = jnp.mean(memory * memory, axis=1, keepdims=True)
    memory_part = memory * lax.rsqrt(mean + epsilon) * gain_ref[...]
    out_ref[0] = (attention_ref[...] + memory_part).astype(jnp.bfloat16)


def call(kernel, shape, flops, *args):
    return pl.pallas_call(
        kernel,
        out_shape=jax.ShapeDtypeStruct(shape, jnp.bfloat16),
        in_specs=[SMEM] + [VMEM] * (len(args) - 1),
        out_specs=VMEM,
        compiler_params=pltpu.CompilerParams(vmem_limit_bytes=32 * 2**20),
        cost_estimate=pl.CostEstimate(
            flops=flops, bytes_accessed=2**20, transcendentals=2**17
        ),
    )(*args)


def on_device(
    queries,
    key_vectors,
    value_vectors,
    token_rate,
    fast_gate,
    fast_up,
    fast_down,
    attention_gain,
    memory_gain,
):
    keys, values = key_vectors[0], value_vectors[0]
    head_depth = keys.shape[1]
    hidden_units = fast_gate.shape[1]
    core = lax.axis_index(PAIR)
    core_vector = core.reshape(1)
    index = lax.axis_index(TOK)
    has_outer = jnp.where(core == 0, index > 0, index < lax.axis_size(TOK) - 1)

    scaled = (token_rate[0][:, None] * values.astype(jnp.float32)).astype(jnp.bfloat16)
    own = jnp.stack([keys, scaled, values])
    partner = from_partner(own)
    half = hidden_units // 2
    grads = call(
        gradient_kernel,
        (half, 3 * head_depth),
        2**30,
        core_vector,
        own,
        partner,
        fast_gate,
        fast_up,
        fast_down,
    )
    near = lax.axis_size(NEAR)
    tiles = grads.reshape(near, half // near, 3 * head_depth)
    arrived = exchange(tiles, NEAR)
    sums = jnp.sum(arrived.astype(jnp.float32), axis=0).astype(jnp.bfloat16)
    sums = jnp.sum(copies_to(sums, FAR).astype(jnp.float32), axis=0).astype(jnp.bfloat16)
    own_sum = copies_to(sums, NEAR).reshape(half, 3 * head_depth)
    partner_sum = from_partner(own_sum)

    outer = outer_halo(keys, values, core)
    attended = window_attention(
        queries[0], keys, values, partner[0], partner[2], outer, core, has_outer
    )
    squares = jnp.sum(attended * attended, axis=1)
    width_sum = head_sum(squares)
    width_mean = width_sum / (lax.axis_size("head") * head_depth)
    attention_part = attended * lax.rsqrt(width_mean + epsilon)[:, None] * attention_gain

    return call(
        renew_kernel,
        queries.shape,
        3 * 2**30,
        core_vector,
        own_sum,
        partner_sum,
        fast_gate,
        fast_up,
        fast_down,
        queries,
        attention_part,
        memory_gain,
    )


def solution(mesh):
    finer = Mesh(
        mesh.devices.reshape(4, 4, 4, 2, mesh.shape["head"]), ("y", "zh", "zl", "c", "head")
    )
    return jax.shard_map(
        on_device,
        mesh=finer,
        in_specs=(
            P("head", TOK, None),
            P("head", TOK, None),
            P("head", TOK, None),
            P("head", TOK),
            P("head", None, None),
            P("head", None, None),
            P("head", None, None),
            P("head", None),
            P("head", None),
        ),
        out_specs=P("head", TOK, None),
        check_vma=False,
    )
```

```python
import functools

import jax
import jax.numpy as jnp
from jax import lax
from jax.experimental import pallas as pl
from jax.experimental.pallas import tpu as pltpu
from jax.sharding import Mesh
from jax.sharding import PartitionSpec as P


HALO = 128
NS_STEPS = 2
TOK = ("y", "zh", "zl", "c")
NEAR = ("y", "zl")
FAR = "zh"
PAIR = "c"
FAR_ORDER = [[2, 3, 0, 1]]

first_coeff = 3.4445
second_coeff = -4.775
third_coefficient = 2.0315
step_size = 1.0
norm_floor = 1e-07
epsilon = 1e-06
masked_score = -1e30

VMEM = pl.BlockSpec(memory_space=pltpu.VMEM)
SMEM = pl.BlockSpec(memory_space=pltpu.SMEM)
HBM = pl.BlockSpec(memory_space=pltpu.HBM)


def dot(a, b, dims):
    return lax.dot_general(a, b, (dims, ((), ())), preferred_element_type=jnp.float32)


def outer_halo(keys, values, core):
    count = lax.axis_size(TOK)
    ends = range(1, count - 1, 2)
    swap = [(i, i + 1) for i in ends] + [(i + 1, i) for i in ends]
    first = jnp.stack([keys[:HALO], values[:HALO]])
    last = jnp.stack([keys[-HALO:], values[-HALO:]])
    return lax.ppermute(jnp.where(core == 0, first, last), TOK, swap)


def from_partner(array):
    return lax.ppermute(array, PAIR, [(0, 1), (1, 0)])


def exchange(tiles, axis, groups=None):
    return lax.all_to_all(
        tiles, axis, split_axis=0, concat_axis=0, axis_index_groups=groups, tiled=True
    )


def copies_to(array, axis, groups=None):
    copies = jnp.broadcast_to(array, (lax.axis_size(axis), *array.shape))
    return exchange(copies, axis, groups)


def head_sum(partial):
    heads = lax.axis_size("head")
    distance = 1
    while distance < heads:
        pairs = [(i, i ^ distance) for i in range(heads)]
        partial = partial + lax.ppermute(partial, "head", pairs)
        distance *= 2
    return partial


def as_row(column):
    size = column.shape[0]
    diagonal = lax.broadcasted_iota(jnp.int32, (size, size), 0) == lax.broadcasted_iota(
        jnp.int32, (size, size), 1
    )
    return jnp.sum(jnp.where(diagonal, column, 0.0), axis=0, keepdims=True)


def as_column(row):
    size = row.shape[1]
    diagonal = lax.broadcasted_iota(jnp.int32, (size, size), 0) == lax.broadcasted_iota(
        jnp.int32, (size, size), 1
    )
    return jnp.sum(jnp.where(diagonal, row, 0.0), axis=1, keepdims=True)


def prepare_kernel(
    core_ref,
    keys_ref,
    values_ref,
    rate_ref,
    gate_ref,
    up_ref,
    down_ref,
    out_ref,
    weights_ref,
    rate,
    semaphores,
):
    half = weights_ref.shape[1]
    mine = pl.ds(pl.multiple_of(core_ref[0] * half, half), half)
    copies = [
        pltpu.make_async_copy(rate_ref, rate, semaphores.at[0]),
        pltpu.make_async_copy(values_ref.at[0], out_ref.at[2], semaphores.at[1]),
        pltpu.make_async_copy(keys_ref.at[0], out_ref.at[0], semaphores.at[2]),
    ]
    for i, ref in enumerate((gate_ref, up_ref, down_ref)):
        copies.append(
            pltpu.make_async_copy(ref.at[0, mine], weights_ref.at[i], semaphores.at[3 + i])
        )
    for copy in copies:
        copy.start()
    copies[0].wait()
    column = as_column(rate[...])
    copies[1].wait()
    out_ref[1] = (column * out_ref[2].astype(jnp.float32)).astype(jnp.bfloat16)
    for copy in copies[2:]:
        copy.wait()


def attention_kernel(
    core_ref, has_outer_ref, queries_ref, own_ref, partner_ref, outer_ref, out_ref, squares_ref
):
    near = pl.ds(pl.multiple_of(core_ref[0] * HALO, HALO), HALO)
    queries = queries_ref[0]
    scale = queries.shape[1] ** (-0.5)
    keys = (own_ref[0], partner_ref[0, near], outer_ref[0])
    values = (own_ref[2], partner_ref[2, near], outer_ref[1])
    scores = [dot(queries, k, ((1,), (1,))) * scale for k in keys]
    scores[2] = jnp.where(has_outer_ref[0] > 0, scores[2], masked_score)
    highest = functools.reduce(jnp.maximum, [jnp.max(s, axis=1, keepdims=True) for s in scores])
    weights = [jnp.exp(s - highest) for s in scores]
    total = sum(jnp.sum(w, axis=1, keepdims=True) for w in weights)
    attended = 0.0
    for w, v in zip(weights, values):
        attended += dot((w / total).astype(jnp.bfloat16), v, ((1,), (0,)))
    out_ref[...] = attended
    squares_ref[...] = as_row(jnp.sum(attended * attended, axis=1, keepdims=True))


def gradient_kernel(own_ref, partner_ref, weights_ref, out_ref):
    depth = weights_ref.shape[2]
    keys = jnp.concatenate([own_ref[0], partner_ref[0]], axis=0)
    scaled = jnp.concatenate([own_ref[1], partner_ref[1]], axis=0)
    gate_value = dot(keys, weights_ref[0], ((1,), (1,)))
    up_value = dot(keys, weights_ref[1], ((1,), (1,)))
    backward = dot(scaled, weights_ref[2], ((1,), (1,)))
    squashed = jax.nn.sigmoid(gate_value)
    silu = gate_value * squashed
    hidden = (silu * up_value).astype(jnp.bfloat16)
    gate_grad = (backward * up_value * squashed * (1.0 + gate_value * (1.0 - squashed))).astype(
        jnp.bfloat16
    )
    up_grad = (backward * silu).astype(jnp.bfloat16)
    pairs = ((gate_grad, keys), (up_grad, keys), (hidden, scaled))
    for i, (left, right) in enumerate(pairs):
        total = dot(left, right, ((0,), (0,)))
        out_ref[:, i * depth : (i + 1) * depth] = total.astype(jnp.bfloat16)


def renew_kernel(
    width,
    core_ref,
    own_ref,
    partner_ref,
    gate_ref,
    up_ref,
    down_ref,
    queries_ref,
    attended_ref,
    width_ref,
    attention_gain_ref,
    memory_gain_ref,
    out_ref,
    gains,
    semaphores,
):
    gain_copies = [
        pltpu.make_async_copy(ref, gains.at[i], semaphores.at[i])
        for i, ref in enumerate((attention_gain_ref, memory_gain_ref))
    ]
    for copy in gain_copies:
        copy.start()
    half = own_ref.shape[0]
    depth = gate_ref.shape[2]
    core = core_ref[0]
    rows = [pl.ds(pl.multiple_of(c * half, half), half) for c in (core, 1 - core)]
    diagonal = lax.broadcasted_iota(jnp.int32, (depth, depth), 0) == lax.broadcasted_iota(
        jnp.int32, (depth, depth), 1
    )
    current, rounded, grams = [], [], []
    for i in range(3):
        grads = jnp.concatenate(
            [ref[:, i * depth : (i + 1) * depth] for ref in (own_ref, partner_ref)], axis=0
        )
        gram = dot(grads, grads, ((0,), (0,)))
        trace = jnp.sum(jnp.where(diagonal, gram, 0.0), axis=0, keepdims=True)
        norm = jnp.sqrt(jnp.sum(trace, axis=1, keepdims=True))
        scaling = 1.0 / (norm + norm_floor)
        current.append(grads.astype(jnp.float32) * scaling)
        rounded.append(current[i].astype(jnp.bfloat16))
        grams.append(gram * scaling * scaling)
    for step in range(NS_STEPS):
        if step:
            grams = [dot(r, r, ((0,), (0,))) for r in rounded]
        mixers = []
        for gram in grams:
            low = gram.astype(jnp.bfloat16)
            squared = dot(low, low, ((1,), (0,)))
            mixers.append((second_coeff * gram + third_coefficient * squared).astype(jnp.bfloat16))
        current = [
            first_coeff * c + dot(r, m, ((1,), (0,))) for c, r, m in zip(current, rounded, mixers)
        ]
        rounded = [c.astype(jnp.bfloat16) for c in current]
    renewed = []
    for weights_ref, update in zip((gate_ref, up_ref, down_ref), current):
        weights = jnp.concatenate([weights_ref[0, r] for r in rows], axis=0).astype(jnp.float32)
        renewed.append((weights + step_size * update).astype(jnp.bfloat16))
    queries = queries_ref[0]
    gate_value = dot(queries, renewed[0], ((1,), (1,)))
    up_value = dot(queries, renewed[1], ((1,), (1,)))
    hidden = (gate_value * jax.nn.sigmoid(gate_value) * up_value).astype(jnp.bfloat16)
    memory = dot(hidden, renewed[2], ((1,), (0,)))
    mean = jnp.mean(memory * memory, axis=1, keepdims=True)
    width_scale = as_column(lax.rsqrt(width_ref[...] / width + epsilon))
    for copy in gain_copies:
        copy.wait()
    attention_part = attended_ref[...] * width_scale * gains[0]
    memory_part = memory * lax.rsqrt(mean + epsilon) * gains[1]
    out_ref[0] = (attention_part + memory_part).astype(jnp.bfloat16)


def in_hbm(*arrays):
    return [pltpu.with_memory_space_constraint(a, pltpu.HBM) for a in arrays]


def call(kernel, shapes, specs, flops, args, scratch=()):
    return pl.pallas_call(
        kernel,
        out_shape=shapes,
        in_specs=specs,
        out_specs=jax.tree.map(lambda _: VMEM, shapes),
        scratch_shapes=scratch,
        compiler_params=pltpu.CompilerParams(vmem_limit_bytes=32 * 2**20),
        cost_estimate=pl.CostEstimate(flops=flops, bytes_accessed=2**20, transcendentals=2**17),
    )(*args)


def on_device(
    queries,
    key_vectors,
    value_vectors,
    token_rate,
    fast_gate,
    fast_up,
    fast_down,
    attention_gain,
    memory_gain,
):
    rows, head_depth = key_vectors.shape[1:]
    hidden_units = fast_gate.shape[1]
    core = lax.axis_index(PAIR)
    core_vector = core.reshape(1)
    index = lax.axis_index(TOK)
    has_outer = jnp.where(core == 0, index > 0, index < lax.axis_size(TOK) - 1)
    narrow = functools.partial(jax.ShapeDtypeStruct, dtype=jnp.bfloat16)
    wide = functools.partial(jax.ShapeDtypeStruct, dtype=jnp.float32)

    half = hidden_units // 2
    own, weights = call(
        prepare_kernel,
        (narrow((3, rows, head_depth)), narrow((3, half, head_depth))),
        [SMEM] + [HBM] * 6,
        2**20,
        (
            core_vector,
            *in_hbm(key_vectors, value_vectors, token_rate, fast_gate, fast_up, fast_down),
        ),
        [pltpu.VMEM((1, rows), jnp.float32), pltpu.SemaphoreType.DMA((6,))],
    )
    partner = from_partner(own)
    grads = call(
        gradient_kernel, narrow((half, 3 * head_depth)), [VMEM] * 3, 2**30, (own, partner, weights)
    )
    near = lax.axis_size(NEAR)
    tiles = grads.reshape(near, half // near, 3 * head_depth)
    arrived = exchange(tiles, NEAR)
    sums = jnp.sum(arrived.astype(jnp.float32), axis=0).astype(jnp.bfloat16)
    arrived = copies_to(sums, FAR, FAR_ORDER)
    sums = jnp.sum(arrived.astype(jnp.float32), axis=0).astype(jnp.bfloat16)
    own_sum = copies_to(sums, NEAR).reshape(half, 3 * head_depth)
    partner_sum = from_partner(own_sum)

    outer = outer_halo(own[0], own[2], core)
    attended, squares = call(
        attention_kernel,
        (wide((rows, head_depth)), wide((1, rows))),
        [SMEM] * 2 + [VMEM] * 4,
        2**28,
        (core_vector, has_outer.astype(jnp.int32).reshape(1), queries, own, partner, outer),
    )
    width_sum = head_sum(squares)

    return call(
        functools.partial(renew_kernel, lax.axis_size("head") * head_depth),
        narrow(queries.shape),
        [SMEM] + [VMEM] * 8 + [HBM] * 2,
        3 * 2**30,
        (
            core_vector,
            own_sum,
            partner_sum,
            fast_gate,
            fast_up,
            fast_down,
            queries,
            attended,
            width_sum,
            *in_hbm(attention_gain, memory_gain),
        ),
        [pltpu.VMEM((2, 1, head_depth), jnp.float32), pltpu.SemaphoreType.DMA((2,))],
    )


def solution(mesh):
    finer = Mesh(
        mesh.devices.reshape(4, 4, 4, 2, mesh.shape["head"]), ("y", "zh", "zl", "c", "head")
    )
    return jax.shard_map(
        on_device,
        mesh=finer,
        in_specs=(
            P("head", TOK, None),
            P("head", TOK, None),
            P("head", TOK, None),
            P("head", TOK),
            P("head", None, None),
            P("head", None, None),
            P("head", None, None),
            P("head", None),
            P("head", None),
        ),
        out_specs=P("head", TOK, None),
        check_vma=False,
    )
```

```python
import functools

import jax
import jax.numpy as jnp
from jax import lax
from jax.experimental import pallas as pl
from jax.experimental.pallas import tpu as pltpu
from jax.sharding import Mesh
from jax.sharding import PartitionSpec as P


HALO = 128
NS_STEPS = 2
TOK = ("y", "zh", "zl", "c")
NEAR = ("y", "zl")
FAR = "zh"
PAIR = "c"
FAR_ORDER = [[2, 3, 0, 1]]
NEAR_ORDER = [[(i + 8) % 16 for i in range(16)]]

first_coeff = 3.4445
second_coeff = -4.775
third_coefficient = 2.0315
step_size = 1.0
norm_floor = 1e-07
epsilon = 1e-06
masked_score = -1e30

VMEM = pl.BlockSpec(memory_space=pltpu.VMEM)
SMEM = pl.BlockSpec(memory_space=pltpu.SMEM)
HBM = pl.BlockSpec(memory_space=pltpu.HBM)


def dot(a, b, dims):
    return lax.dot_general(a, b, (dims, ((), ())), preferred_element_type=jnp.float32)


def outer_halo(keys, values, core):
    count = lax.axis_size(TOK)
    ends = range(1, count - 1, 2)
    swap = [(i, i + 1) for i in ends] + [(i + 1, i) for i in ends]
    first = jnp.stack([keys[:HALO], values[:HALO]])
    last = jnp.stack([keys[-HALO:], values[-HALO:]])
    return lax.ppermute(jnp.where(core == 0, first, last), TOK, swap)


def from_partner(array):
    return lax.ppermute(array, PAIR, [(0, 1), (1, 0)])


def exchange(tiles, axis, groups=None):
    return lax.all_to_all(
        tiles, axis, split_axis=0, concat_axis=0, axis_index_groups=groups, tiled=True
    )


def copies_to(array, axis, groups=None):
    copies = jnp.broadcast_to(array, (lax.axis_size(axis), *array.shape))
    return exchange(copies, axis, groups)


def head_sum(partial):
    heads = lax.axis_size("head")
    step = 1
    while 2**step <= heads:
        pairs = [(i, i ^ (2**step - 1)) for i in range(heads)]
        partial = partial + lax.ppermute(partial, "head", pairs)
        step += 1
    return partial


def as_row(column):
    size = column.shape[0]
    diagonal = lax.broadcasted_iota(jnp.int32, (size, size), 0) == lax.broadcasted_iota(
        jnp.int32, (size, size), 1
    )
    return jnp.sum(jnp.where(diagonal, column, 0.0), axis=0, keepdims=True)


def as_column(row):
    size = row.shape[1]
    diagonal = lax.broadcasted_iota(jnp.int32, (size, size), 0) == lax.broadcasted_iota(
        jnp.int32, (size, size), 1
    )
    return jnp.sum(jnp.where(diagonal, row, 0.0), axis=1, keepdims=True)


def prepare_kernel(
    core_ref,
    keys_ref,
    values_ref,
    rate_ref,
    gate_ref,
    up_ref,
    down_ref,
    out_ref,
    weights_ref,
    rate,
    semaphores,
):
    half = weights_ref.shape[1]
    mine = pl.ds(pl.multiple_of(core_ref[0] * half, half), half)
    copies = [
        pltpu.make_async_copy(rate_ref, rate, semaphores.at[0]),
        pltpu.make_async_copy(values_ref.at[0], out_ref.at[2], semaphores.at[1]),
        pltpu.make_async_copy(keys_ref.at[0], out_ref.at[0], semaphores.at[2]),
    ]
    for i, ref in enumerate((gate_ref, up_ref, down_ref)):
        copies.append(
            pltpu.make_async_copy(ref.at[0, mine], weights_ref.at[i], semaphores.at[3 + i])
        )
    for copy in copies:
        copy.start()
    copies[0].wait()
    column = as_column(rate[...])
    copies[1].wait()
    out_ref[1] = (column * out_ref[2].astype(jnp.float32)).astype(jnp.bfloat16)
    for copy in copies[2:]:
        copy.wait()


def attention_kernel(
    core_ref,
    has_outer_ref,
    queries_ref,
    own_ref,
    partner_ref,
    outer_ref,
    attention_gain_ref,
    memory_gain_ref,
    out_ref,
    squares_ref,
    gains_ref,
    semaphores,
):
    gain_copies = [
        pltpu.make_async_copy(ref, gains_ref.at[i], semaphores.at[i])
        for i, ref in enumerate((attention_gain_ref, memory_gain_ref))
    ]
    for copy in gain_copies:
        copy.start()
    near = pl.ds(pl.multiple_of(core_ref[0] * HALO, HALO), HALO)
    queries = queries_ref[0]
    scale = queries.shape[1] ** (-0.5)
    keys = (own_ref[0], partner_ref[0, near], outer_ref[0])
    values = (own_ref[2], partner_ref[2, near], outer_ref[1])
    scores = [dot(queries, k, ((1,), (1,))) * scale for k in keys]
    scores[2] = jnp.where(has_outer_ref[0] > 0, scores[2], masked_score)
    highest = functools.reduce(jnp.maximum, [jnp.max(s, axis=1, keepdims=True) for s in scores])
    weights = [jnp.exp(s - highest) for s in scores]
    total = sum(jnp.sum(w, axis=1, keepdims=True) for w in weights)
    attended = 0.0
    for w, v in zip(weights, values):
        attended += dot((w / total).astype(jnp.bfloat16), v, ((1,), (0,)))
    out_ref[...] = attended
    squares_ref[...] = as_row(jnp.sum(attended * attended, axis=1, keepdims=True))
    for copy in gain_copies:
        copy.wait()


def signals(keys, scaled, weights_ref):
    gate_value = dot(keys, weights_ref[0], ((1,), (1,)))
    up_value = dot(keys, weights_ref[1], ((1,), (1,)))
    backward = dot(scaled, weights_ref[2], ((1,), (1,)))
    squashed = jax.nn.sigmoid(gate_value)
    silu = gate_value * squashed
    gate_grad = backward * up_value * squashed * (1.0 + gate_value * (1.0 - squashed))
    return [x.astype(jnp.bfloat16) for x in (gate_grad, backward * silu, silu * up_value)]


def signal_kernel(own_ref, weights_ref, out_ref, turned_ref):
    for i, x in enumerate(signals(own_ref[0], own_ref[1], weights_ref)):
        out_ref[i] = x
    for i in range(2):
        turned_ref[i] = own_ref[i].T


def gradient_kernel(partner_ref, weights_ref, signals_ref, turned_ref, out_ref):
    half = weights_ref.shape[1]
    turned = [
        jnp.concatenate([turned_ref[i], partner_ref[i].T], axis=1) for i in range(2)
    ]
    for i, right in enumerate(signals(partner_ref[0], partner_ref[1], weights_ref)):
        total = dot(
            turned[1 if i == 2 else 0],
            jnp.concatenate([signals_ref[i], right], axis=0),
            ((1,), (0,)),
        )
        out_ref[:, i * half : (i + 1) * half] = total.astype(jnp.bfloat16)


def turn_kernel(core_ref, gate_ref, up_ref, down_ref, out_ref):
    half = gate_ref.shape[1] // 2
    core = core_ref[0]
    for i, ref in enumerate((gate_ref, up_ref, down_ref)):
        for j, c in enumerate((core, 1 - core)):
            rows = ref[0, pl.ds(pl.multiple_of(c * half, half), half)]
            out_ref[i, :, j * half : (j + 1) * half] = rows.T


def renew_kernel(
    width,
    own_ref,
    partner_ref,
    turned_ref,
    queries_ref,
    attended_ref,
    width_ref,
    gains_ref,
    out_ref,
):
    depth = own_ref.shape[0]
    half = turned_ref.shape[2] // 2
    diagonal = lax.broadcasted_iota(jnp.int32, (depth, depth), 0) == lax.broadcasted_iota(
        jnp.int32, (depth, depth), 1
    )
    current, rounded, grams = [], [], []
    for i in range(3):
        grads = jnp.concatenate(
            [ref[:, i * half : (i + 1) * half] for ref in (own_ref, partner_ref)], axis=1
        )
        gram = dot(grads, grads, ((1,), (1,)))
        trace = jnp.sum(jnp.where(diagonal, gram, 0.0), axis=0, keepdims=True)
        norm = jnp.sqrt(jnp.sum(trace, axis=1, keepdims=True))
        scaling = 1.0 / (norm + norm_floor)
        current.append(grads.astype(jnp.float32) * scaling)
        rounded.append(current[i].astype(jnp.bfloat16))
        grams.append(gram * scaling * scaling)
    for step in range(NS_STEPS):
        if step:
            grams = [dot(r, r, ((1,), (1,))) for r in rounded]
        mixers = []
        for gram in grams:
            low = gram.astype(jnp.bfloat16)
            squared = dot(low, low, ((1,), (0,)))
            mixers.append((second_coeff * gram + third_coefficient * squared).astype(jnp.bfloat16))
        current = [
            first_coeff * c + dot(m, r, ((1,), (0,))) for c, r, m in zip(current, rounded, mixers)
        ]
        rounded = [c.astype(jnp.bfloat16) for c in current]
    renewed = [
        (turned_ref[i].astype(jnp.float32) + step_size * c).astype(jnp.bfloat16)
        for i, c in enumerate(current)
    ]
    queries = queries_ref[0]
    gate_value = dot(queries, renewed[0], ((1,), (0,)))
    up_value = dot(queries, renewed[1], ((1,), (0,)))
    hidden = (gate_value * jax.nn.sigmoid(gate_value) * up_value).astype(jnp.bfloat16)
    memory = dot(hidden, renewed[2], ((1,), (1,)))
    mean = jnp.mean(memory * memory, axis=1, keepdims=True)
    width_scale = as_column(lax.rsqrt(width_ref[...] / width + epsilon))
    attention_part = attended_ref[...] * width_scale * gains_ref[0]
    memory_part = memory * lax.rsqrt(mean + epsilon) * gains_ref[1]
    out_ref[0] = (attention_part + memory_part).astype(jnp.bfloat16)


def in_hbm(*arrays):
    return [pltpu.with_memory_space_constraint(a, pltpu.HBM) for a in arrays]


def call(kernel, shapes, specs, flops, args, scratch=()):
    return pl.pallas_call(
        kernel,
        out_shape=shapes,
        in_specs=specs,
        out_specs=jax.tree.map(lambda _: VMEM, shapes),
        scratch_shapes=scratch,
        compiler_params=pltpu.CompilerParams(vmem_limit_bytes=32 * 2**20),
        cost_estimate=pl.CostEstimate(flops=flops, bytes_accessed=2**20, transcendentals=2**17),
    )(*args)


def on_device(
    queries,
    key_vectors,
    value_vectors,
    token_rate,
    fast_gate,
    fast_up,
    fast_down,
    attention_gain,
    memory_gain,
):
    rows, head_depth = key_vectors.shape[1:]
    hidden_units = fast_gate.shape[1]
    core = lax.axis_index(PAIR)
    core_vector = core.reshape(1)
    index = lax.axis_index(TOK)
    has_outer = jnp.where(core == 0, index > 0, index < lax.axis_size(TOK) - 1)
    narrow = functools.partial(jax.ShapeDtypeStruct, dtype=jnp.bfloat16)
    wide = functools.partial(jax.ShapeDtypeStruct, dtype=jnp.float32)

    half = hidden_units // 2
    own, weights = call(
        prepare_kernel,
        (narrow((3, rows, head_depth)), narrow((3, half, head_depth))),
        [SMEM] + [HBM] * 6,
        2**20,
        (
            core_vector,
            *in_hbm(key_vectors, value_vectors, token_rate, fast_gate, fast_up, fast_down),
        ),
        [pltpu.VMEM((1, rows), jnp.float32), pltpu.SemaphoreType.DMA((6,))],
    )
    partner = from_partner(own)
    own_signals, own_turned = call(
        signal_kernel,
        (narrow((3, rows, half)), narrow((2, head_depth, rows))),
        [VMEM] * 2,
        2**29,
        (own, weights),
    )
    grads = call(
        gradient_kernel,
        narrow((head_depth, 3 * half)),
        [VMEM] * 4,
        2**30,
        (partner, weights, own_signals, own_turned),
    )
    turned = call(
        turn_kernel,
        narrow((3, head_depth, hidden_units)),
        [SMEM] + [VMEM] * 3,
        2**27,
        (core_vector, fast_gate, fast_up, fast_down),
    )
    near = lax.axis_size(NEAR)
    tiles = grads.reshape(near, head_depth // near, 3 * half)
    arrived = exchange(tiles, NEAR, NEAR_ORDER)
    sums = jnp.sum(arrived.astype(jnp.float32), axis=0).astype(jnp.bfloat16)
    arrived = copies_to(sums, FAR, FAR_ORDER)
    sums = jnp.sum(arrived.astype(jnp.float32), axis=0).astype(jnp.bfloat16)
    own_sum = copies_to(sums, NEAR, NEAR_ORDER).reshape(grads.shape)
    partner_sum = from_partner(own_sum)

    outer = outer_halo(own[0], own[2], core)
    attended, squares, gains = call(
        attention_kernel,
        (wide((rows, head_depth)), wide((1, rows)), wide((2, 1, head_depth))),
        [SMEM] * 2 + [VMEM] * 4 + [HBM] * 2,
        2**28,
        (
            core_vector,
            has_outer.astype(jnp.int32).reshape(1),
            queries,
            own,
            partner,
            outer,
            *in_hbm(attention_gain, memory_gain),
        ),
        [pltpu.SemaphoreType.DMA((2,))],
    )
    width_sum = head_sum(squares)

    return call(
        functools.partial(renew_kernel, lax.axis_size("head") * head_depth),
        narrow(queries.shape),
        [VMEM] * 7,
        3 * 2**30,
        (own_sum, partner_sum, turned, queries, attended, width_sum, gains),
    )


def solution(mesh):
    finer = Mesh(
        mesh.devices.reshape(4, 4, 4, 2, mesh.shape["head"]), ("y", "zh", "zl", "c", "head")
    )
    return jax.shard_map(
        on_device,
        mesh=finer,
        in_specs=(
            P("head", TOK, None),
            P("head", TOK, None),
            P("head", TOK, None),
            P("head", TOK),
            P("head", None, None),
            P("head", None, None),
            P("head", None, None),
            P("head", None),
            P("head", None),
        ),
        out_specs=P("head", TOK, None),
        check_vma=False,
    )
```

```python
import functools

import jax
import jax.numpy as jnp
from jax import lax
from jax.experimental import pallas as pl
from jax.experimental.pallas import tpu as pltpu
from jax.sharding import Mesh
from jax.sharding import PartitionSpec as P


HALO = 128
NS_STEPS = 2
TOK = ("y", "zh", "zl", "c")
NEAR = ("y", "zl")
FAR = "zh"
PAIR = "c"
FAR_ORDER = [[2, 0, 1, 3]]
NEAR_ORDER = [[(y % 4) * 4 + z for y in range(2, 6) for z in (1, 0, 2, 3)]]

first_coeff = 3.4445
second_coeff = -4.775
third_coefficient = 2.0315
step_size = 1.0
norm_floor = 1e-07
epsilon = 1e-06
masked_score = -1e30

VMEM = pl.BlockSpec(memory_space=pltpu.VMEM)
SMEM = pl.BlockSpec(memory_space=pltpu.SMEM)
HBM = pl.BlockSpec(memory_space=pltpu.HBM)


def dot(a, b, dims):
    return lax.dot_general(a, b, (dims, ((), ())), preferred_element_type=jnp.float32)


def outer_halo(keys, values, core):
    count = lax.axis_size(TOK)
    ends = range(1, count - 1, 2)
    swap = [(i, i + 1) for i in ends] + [(i + 1, i) for i in ends]
    first = jnp.stack([keys[:HALO], values[:HALO]])
    last = jnp.stack([keys[-HALO:], values[-HALO:]])
    return lax.ppermute(jnp.where(core == 0, first, last), TOK, swap)


def from_partner(array):
    return lax.ppermute(array, PAIR, [(0, 1), (1, 0)])


def exchange(tiles, axis, groups=None):
    return lax.all_to_all(
        tiles, axis, split_axis=0, concat_axis=0, axis_index_groups=groups, tiled=True
    )


def head_sum(partial):
    heads = lax.axis_size("head")
    step = 1
    while 2**step <= heads:
        pairs = [(i, i ^ (2**step - 1)) for i in range(heads)]
        partial = partial + lax.ppermute(partial, "head", pairs)
        step += 1
    return partial


def as_row(column):
    size = column.shape[0]
    diagonal = lax.broadcasted_iota(jnp.int32, (size, size), 0) == lax.broadcasted_iota(
        jnp.int32, (size, size), 1
    )
    return jnp.sum(jnp.where(diagonal, column, 0.0), axis=0, keepdims=True)


def as_column(row):
    size = row.shape[1]
    diagonal = lax.broadcasted_iota(jnp.int32, (size, size), 0) == lax.broadcasted_iota(
        jnp.int32, (size, size), 1
    )
    return jnp.sum(jnp.where(diagonal, row, 0.0), axis=1, keepdims=True)


def prepare_kernel(
    core_ref,
    keys_ref,
    values_ref,
    rate_ref,
    gate_ref,
    up_ref,
    down_ref,
    out_ref,
    weights_ref,
    rate,
    semaphores,
):
    half = weights_ref.shape[1]
    mine = pl.ds(pl.multiple_of(core_ref[0] * half, half), half)
    copies = [
        pltpu.make_async_copy(rate_ref, rate, semaphores.at[0]),
        pltpu.make_async_copy(values_ref.at[0], out_ref.at[2], semaphores.at[1]),
        pltpu.make_async_copy(keys_ref.at[0], out_ref.at[0], semaphores.at[2]),
    ]
    for i, ref in enumerate((gate_ref, up_ref, down_ref)):
        copies.append(
            pltpu.make_async_copy(ref.at[0, mine], weights_ref.at[i], semaphores.at[3 + i])
        )
    for copy in copies:
        copy.start()
    copies[0].wait()
    column = as_column(rate[...])
    copies[1].wait()
    out_ref[1] = (column * out_ref[2].astype(jnp.float32)).astype(jnp.bfloat16)
    for copy in copies[2:]:
        copy.wait()


def attention_kernel(
    core_ref,
    has_outer_ref,
    queries_ref,
    own_ref,
    partner_ref,
    outer_ref,
    attention_gain_ref,
    memory_gain_ref,
    out_ref,
    squares_ref,
    gains_ref,
    semaphores,
):
    gain_copies = [
        pltpu.make_async_copy(ref, gains_ref.at[i], semaphores.at[i])
        for i, ref in enumerate((attention_gain_ref, memory_gain_ref))
    ]
    for copy in gain_copies:
        copy.start()
    near = pl.ds(pl.multiple_of(core_ref[0] * HALO, HALO), HALO)
    queries = queries_ref[0]
    scale = queries.shape[1] ** (-0.5)
    keys = (own_ref[0], partner_ref[0, near], outer_ref[0])
    values = (own_ref[2], partner_ref[2, near], outer_ref[1])
    scores = [dot(queries, k, ((1,), (1,))) * scale for k in keys]
    scores[2] = jnp.where(has_outer_ref[0] > 0, scores[2], masked_score)
    highest = functools.reduce(jnp.maximum, [jnp.max(s, axis=1, keepdims=True) for s in scores])
    weights = [jnp.exp(s - highest) for s in scores]
    total = sum(jnp.sum(w, axis=1, keepdims=True) for w in weights)
    attended = 0.0
    for w, v in zip(weights, values):
        attended += dot((w / total).astype(jnp.bfloat16), v, ((1,), (0,)))
    out_ref[...] = attended
    squares_ref[...] = as_row(jnp.sum(attended * attended, axis=1, keepdims=True))
    for copy in gain_copies:
        copy.wait()


def sum_kernel(arrived_ref, out_ref):
    total = jnp.sum(arrived_ref[...].astype(jnp.float32), axis=0).astype(jnp.bfloat16)
    for i in range(out_ref.shape[0]):
        out_ref[i] = total


def signals(keys, scaled, weights_ref):
    gate_value = dot(keys, weights_ref[0], ((1,), (1,)))
    up_value = dot(keys, weights_ref[1], ((1,), (1,)))
    backward = dot(scaled, weights_ref[2], ((1,), (1,)))
    squashed = jax.nn.sigmoid(gate_value)
    silu = gate_value * squashed
    gate_grad = backward * up_value * squashed * (1.0 + gate_value * (1.0 - squashed))
    return [x.astype(jnp.bfloat16) for x in (gate_grad, backward * silu, silu * up_value)]


def gradient_sums(tokens_ref, weights_ref):
    keys, scaled = tokens_ref[0], tokens_ref[1]
    turned = (keys.T, scaled.T)
    for i, right in enumerate(signals(keys, scaled, weights_ref)):
        yield i, dot(turned[1 if i == 2 else 0], right, ((1,), (0,)))


def own_kernel(own_ref, weights_ref, out_ref):
    half = weights_ref.shape[1]
    for i, total in gradient_sums(own_ref, weights_ref):
        out_ref[:, i * half : (i + 1) * half] = total


def gradient_kernel(partner_ref, weights_ref, own_sums_ref, out_ref):
    half = weights_ref.shape[1]
    for i, total in gradient_sums(partner_ref, weights_ref):
        columns = slice(i * half, (i + 1) * half)
        out_ref[:, columns] = (own_sums_ref[:, columns] + total).astype(jnp.bfloat16)


def turn_kernel(core_ref, gate_ref, up_ref, down_ref, out_ref):
    half = gate_ref.shape[1] // 2
    core = core_ref[0]
    for i, ref in enumerate((gate_ref, up_ref, down_ref)):
        for j, c in enumerate((core, 1 - core)):
            rows = ref[0, pl.ds(pl.multiple_of(c * half, half), half)]
            out_ref[i, :, j * half : (j + 1) * half] = rows.T


def renew_kernel(
    width,
    own_ref,
    partner_ref,
    turned_ref,
    queries_ref,
    attended_ref,
    width_ref,
    gains_ref,
    out_ref,
):
    depth = own_ref.shape[0]
    half = turned_ref.shape[2] // 2
    diagonal = lax.broadcasted_iota(jnp.int32, (depth, depth), 0) == lax.broadcasted_iota(
        jnp.int32, (depth, depth), 1
    )
    current, rounded, grams = [], [], []
    for i in range(3):
        grads = jnp.concatenate(
            [ref[:, i * half : (i + 1) * half] for ref in (own_ref, partner_ref)], axis=1
        )
        gram = dot(grads, grads, ((1,), (1,)))
        trace = jnp.sum(jnp.where(diagonal, gram, 0.0), axis=0, keepdims=True)
        norm = jnp.sqrt(jnp.sum(trace, axis=1, keepdims=True))
        scaling = 1.0 / (norm + norm_floor)
        current.append(grads.astype(jnp.float32) * scaling)
        rounded.append(current[i].astype(jnp.bfloat16))
        grams.append(gram * scaling * scaling)
    for step in range(NS_STEPS):
        if step:
            grams = [dot(r, r, ((1,), (1,))) for r in rounded]
        mixers = []
        for gram in grams:
            low = gram.astype(jnp.bfloat16)
            squared = dot(low, low, ((1,), (0,)))
            mixers.append((second_coeff * gram + third_coefficient * squared).astype(jnp.bfloat16))
        current = [
            first_coeff * c + dot(m, r, ((1,), (0,))) for c, r, m in zip(current, rounded, mixers)
        ]
        rounded = [c.astype(jnp.bfloat16) for c in current]
    renewed = [
        (turned_ref[i].astype(jnp.float32) + step_size * c).astype(jnp.bfloat16)
        for i, c in enumerate(current)
    ]
    queries = queries_ref[0]
    gate_value = dot(queries, renewed[0], ((1,), (0,)))
    up_value = dot(queries, renewed[1], ((1,), (0,)))
    hidden = (gate_value * jax.nn.sigmoid(gate_value) * up_value).astype(jnp.bfloat16)
    memory = dot(hidden, renewed[2], ((1,), (1,)))
    mean = jnp.mean(memory * memory, axis=1, keepdims=True)
    width_scale = as_column(lax.rsqrt(width_ref[...] / width + epsilon))
    attention_part = attended_ref[...] * width_scale * gains_ref[0]
    memory_part = memory * lax.rsqrt(mean + epsilon) * gains_ref[1]
    out_ref[0] = (attention_part + memory_part).astype(jnp.bfloat16)


def in_hbm(*arrays):
    return [pltpu.with_memory_space_constraint(a, pltpu.HBM) for a in arrays]


def call(kernel, shapes, specs, flops, args, scratch=()):
    return pl.pallas_call(
        kernel,
        out_shape=shapes,
        in_specs=specs,
        out_specs=jax.tree.map(lambda _: VMEM, shapes),
        scratch_shapes=scratch,
        compiler_params=pltpu.CompilerParams(vmem_limit_bytes=32 * 2**20),
        cost_estimate=pl.CostEstimate(flops=flops, bytes_accessed=2**20, transcendentals=2**17),
    )(*args)


def on_device(
    queries,
    key_vectors,
    value_vectors,
    token_rate,
    fast_gate,
    fast_up,
    fast_down,
    attention_gain,
    memory_gain,
):
    rows, head_depth = key_vectors.shape[1:]
    hidden_units = fast_gate.shape[1]
    core = lax.axis_index(PAIR)
    core_vector = core.reshape(1)
    index = lax.axis_index(TOK)
    has_outer = jnp.where(core == 0, index > 0, index < lax.axis_size(TOK) - 1)
    narrow = functools.partial(jax.ShapeDtypeStruct, dtype=jnp.bfloat16)
    wide = functools.partial(jax.ShapeDtypeStruct, dtype=jnp.float32)

    half = hidden_units // 2
    own, weights = call(
        prepare_kernel,
        (narrow((3, rows, head_depth)), narrow((3, half, head_depth))),
        [SMEM] + [HBM] * 6,
        2**20,
        (
            core_vector,
            *in_hbm(key_vectors, value_vectors, token_rate, fast_gate, fast_up, fast_down),
        ),
        [pltpu.VMEM((1, rows), jnp.float32), pltpu.SemaphoreType.DMA((6,))],
    )
    partner = from_partner(own)
    own_gradients = call(
        own_kernel, wide((head_depth, 3 * half)), [VMEM] * 2, 2**29, (own, weights)
    )
    grads = call(
        gradient_kernel,
        narrow((head_depth, 3 * half)),
        [VMEM] * 3,
        2**29,
        (partner, weights, own_gradients),
    )
    turned = call(
        turn_kernel,
        narrow((3, head_depth, hidden_units)),
        [SMEM] + [VMEM] * 3,
        2**27,
        (core_vector, fast_gate, fast_up, fast_down),
    )
    near = lax.axis_size(NEAR)
    tiles = grads.reshape(near, head_depth // near, 3 * half)
    arrived = exchange(tiles, NEAR, NEAR_ORDER)
    tile = tiles.shape[1:]
    copies = call(sum_kernel, narrow((lax.axis_size(FAR), *tile)), [VMEM], 2**20, (arrived,))
    arrived = exchange(copies, FAR, FAR_ORDER)
    copies = call(sum_kernel, narrow((near, *tile)), [VMEM], 2**20, (arrived,))
    own_sum = exchange(copies, NEAR, NEAR_ORDER).reshape(grads.shape)
    partner_sum = from_partner(own_sum)

    outer = outer_halo(own[0], own[2], core)
    attended, squares, gains = call(
        attention_kernel,
        (wide((rows, head_depth)), wide((1, rows)), wide((2, 1, head_depth))),
        [SMEM] * 2 + [VMEM] * 4 + [HBM] * 2,
        2**28,
        (
            core_vector,
            has_outer.astype(jnp.int32).reshape(1),
            queries,
            own,
            partner,
            outer,
            *in_hbm(attention_gain, memory_gain),
        ),
        [pltpu.SemaphoreType.DMA((2,))],
    )
    width_sum = head_sum(squares)

    return call(
        functools.partial(renew_kernel, lax.axis_size("head") * head_depth),
        narrow(queries.shape),
        [VMEM] * 7,
        3 * 2**30,
        (own_sum, partner_sum, turned, queries, attended, width_sum, gains),
    )


def solution(mesh):
    finer = Mesh(
        mesh.devices.reshape(4, 4, 4, 2, mesh.shape["head"]), ("y", "zh", "zl", "c", "head")
    )
    return jax.shard_map(
        on_device,
        mesh=finer,
        in_specs=(
            P("head", TOK, None),
            P("head", TOK, None),
            P("head", TOK, None),
            P("head", TOK),
            P("head", None, None),
            P("head", None, None),
            P("head", None, None),
            P("head", None),
            P("head", None),
        ),
        out_specs=P("head", TOK, None),
        check_vma=False,
    )
```
